32 devices in a mesh: seq: 8 (over z, y), tensor: 4 (over x, core).
Axes of the slice: x: 2, y: 2, z: 4, core: 2. Of those that a mesh axis runs over, the one named last changes fastest.
Arguments:
- queries: bfloat16 [2048, 4096], P('seq', 'tensor'), may hold values from -12 to 12
- keys: bfloat16 [2048, 512], P('seq', 'tensor'), may hold values from -6 to 6
- values: bfloat16 [2048, 512], P('seq', 'tensor'), may hold values from -6 to 6
- mem_queries: bfloat16 [128, 4096], P(None, 'tensor'), may hold values from -12 to 12
- mem_proj: bfloat16 [1024, 4096], P(None, 'tensor'), may hold values from -0.09375 to 0.09375
- mem_decay: float32 [8, 1024], P('seq', 'tensor'), may hold values from 0 to 1
- pattern: int32 [8, 2, 3], P('seq'), may hold values from 0 to 1, as said below
- grad_out: bfloat16 [2048, 4096], P('seq', 'tensor'), may hold values from -6 to 6
Outputs:
- attn_out: bfloat16 [2048, 4096], P('seq', 'tensor')
- grad_queries: bfloat16 [2048, 4096], P('seq', 'tensor')
- grad_keys: bfloat16 [2048, 512], P('seq', 'tensor')
- grad_values: bfloat16 [2048, 512], P('seq', 'tensor')
The draws below stay inside these ranges and needn't reach their ends.
Inputs may be any that keep to these rules, and one draw needn't show every extreme that they name: pattern[s, b, 0] says whether tile b of segment s reads the memory, pattern[s, b, 1 + j] whether it reads key tile j of its own segment; tile j = b is always 1 and tiles j > b are always 0.
All inputs are finite; a program needn't handle non-finite values.
Results may differ from the reference program's by a relative error of at most 0.0085.
Values sent between devices are 32-bit elements; how exact they have to be, the bound alone decides.
A program may use at most 192 MiB of HBM per device.

```python
import math
import jax
import jax.numpy as jnp
from jax import lax

SEG = 256
H = 32
KVH = 4
HD = 128
MEM = 128
BLOCK = 128
SEGS = 8
TOKENS = 2048


def draw_keys(key, part):
    base_draw = jnp.clip(jax.random.normal(jax.random.fold_in(key, 11), (TOKENS, KVH * HD), jnp.float32), -6.0, 6.0)
    return base_draw.astype(jnp.bfloat16)


def draw_queries(key, part):
    base_draw = jnp.clip(jax.random.normal(jax.random.fold_in(key, 13), (TOKENS, H * HD), jnp.float32), -6.0, 6.0)
    return base_draw.astype(jnp.bfloat16)


def draw_mem_queries(key, part):
    base_draw = jnp.clip(jax.random.normal(jax.random.fold_in(key, 17), (MEM, H * HD), jnp.float32), -6.0, 6.0)
    return base_draw.astype(jnp.bfloat16)


def draw_mem_decay(key, part):
    channels = 2 * KVH * HD
    length_total = SEGS
    key_a, key_b, key_c, key_d, random_key_fifth, random_key_sixth = jax.random.split(jax.random.fold_in(key, 23), 6)
    fast_mask = jax.random.randint(key_a, (channels,), 0, 2) == 0
    slow_rate = jnp.exp(jax.random.uniform(key_b, (channels,), jnp.float32, math.log(0.02), math.log(0.5))) / length_total
    fast_rate = jnp.exp(jax.random.uniform(key_c, (channels,), jnp.float32, math.log(0.5), math.log(3.0)))
    row_rates = jnp.where(fast_mask, fast_rate, slow_rate)
    random_noise = jnp.exp(jax.random.uniform(key_d, (length_total, channels), jnp.float32, math.log(0.5), math.log(2.0)))
    spike_event = jax.random.randint(random_key_fifth, (length_total, 1), 0, length_total) < 3
    spike_retain = jax.random.uniform(random_key_sixth, (length_total, 1), jnp.float32, 0.5, 0.8)
    return jnp.exp(-row_rates[None, :] * random_noise) * jnp.where(spike_event, spike_retain, 1.0)


def draw_pattern(key, part):
    block_count = SEG // BLOCK
    key_a, key_b, key_c = jax.random.split(jax.random.fold_in(key, 31), 3)
    window = jax.random.randint(key_a, (SEGS, 1, 1), 1, block_count + 1)
    sink_bit = jax.random.randint(key_b, (SEGS, 1, 1), 0, 2)
    memory = (jax.random.randint(key_c, (SEGS, block_count, 1), 0, 4) < 3).astype(jnp.int32)
    row_ids = jnp.arange(block_count, dtype=jnp.int32)[None, :, None]
    col_ids = jnp.arange(block_count, dtype=jnp.int32)[None, None, :]
    lower_tri = col_ids <= row_ids
    near_tile = row_ids - col_ids < window
    first_col = (col_ids == 0) & (sink_bit > 0)
    seg_tiles = (lower_tri & (near_tile | first_col)).astype(jnp.int32)
    return jnp.concatenate([memory, seg_tiles], axis=2)


def level_of(stream_key, dims, pieces, low, high):
    gain, own = 1.0, jax.random.fold_in(stream_key, 6)
    for axis_at, parts in pieces:
        steps = jnp.exp(jax.random.uniform(jax.random.fold_in(own, axis_at), (parts,), jnp.float32, low / len(pieces), high / len(pieces)))
        gain = gain * jnp.repeat(steps, dims[axis_at] // parts).reshape([-1 if axis == axis_at else 1 for axis in range(len(dims))])
    return gain


def centred(own_key, dims, deviation, limit, shards=(), kind=jnp.bfloat16):
    values = deviation * jax.random.normal(own_key, dims, jnp.float32)
    if shards:
        values = values * level_of(own_key, dims, shards, -0.22, 0.18)
    return jnp.clip(values, -limit, limit).astype(kind)


def setup_inputs(seed: int = 0) -> dict:
    splits = jax.random.split(jax.random.key(seed), 9)
    queries = draw_queries(jax.random.fold_in(splits[8], 71), 0)
    keys = draw_keys(jax.random.fold_in(splits[8], 71), 0)
    values = centred(splits[2], (TOKENS, KVH * HD), 1.0, 6.0, ((0, 8), (1, 4)))
    mem_queries = draw_mem_queries(jax.random.fold_in(splits[8], 71), 0)
    mem_proj = centred(splits[4], (2 * KVH * HD, H * HD), (H * HD) ** -0.5, 0.09375, ((1, 4),))
    mem_decay = draw_mem_decay(jax.random.fold_in(splits[8], 71), 0)
    pattern = draw_pattern(jax.random.fold_in(splits[8], 71), 0)
    grad_out = centred(splits[7], (TOKENS, H * HD), 1.0, 6.0, ((0, 8), (1, 4)))
    return dict(queries=queries, keys=keys, values=values, mem_queries=mem_queries, mem_proj=mem_proj, mem_decay=mem_decay, pattern=pattern, grad_out=grad_out)


epsilon = 1e-06

def exact_einsum(form, left, right):
    return jnp.einsum(form, left.astype(jnp.float32), right.astype(jnp.float32))

def softmax_rows(scores):
    row_max = lax.optimization_barrier(jnp.max(scores, axis=-1, keepdims=True))
    raised = jnp.exp(scores - row_max)
    return raised / lax.optimization_barrier(jnp.sum(raised, axis=-1, keepdims=True))

def tile_mask(tile_bits, seg_len):
    expanded = jnp.repeat(jnp.repeat(tile_bits, BLOCK, axis=0), BLOCK, axis=1) > 0
    row_ids = jnp.arange(seg_len, dtype=jnp.int32)[:, None]
    col_ids = jnp.arange(MEM + seg_len, dtype=jnp.int32)[None, :]
    causal = (col_ids < MEM) | (col_ids - MEM <= row_ids)
    return expanded & causal

def read_out(mem_queries, seg_keys, seg_values):
    kv_heads = seg_keys.shape[1] // HD
    group_size = mem_queries.shape[1] // HD // kv_heads
    q_grid = mem_queries.reshape(MEM, kv_heads, group_size, HD)
    k_grid = seg_keys.reshape(-1, kv_heads, HD)
    v_grid = seg_values.reshape(-1, kv_heads, HD)
    scores = exact_einsum('qgjd,kgd->gjqk', q_grid, k_grid) * HD ** (-0.5)
    read_probs = softmax_rows(scores)
    read_weights = read_probs.astype(jnp.bfloat16)
    summary = exact_einsum('gjqk,kgd->qgjd', read_weights, v_grid)
    return (summary.reshape(MEM, -1).astype(jnp.bfloat16), read_probs, read_weights)

def read_back(mem_queries, seg_keys, seg_values, read_probs, read_weights, d_summary):
    kv_heads = seg_keys.shape[1] // HD
    group_size = mem_queries.shape[1] // HD // kv_heads
    q_grid = mem_queries.reshape(MEM, kv_heads, group_size, HD)
    v_grid = seg_values.reshape(-1, kv_heads, HD)
    d_grid = d_summary.reshape(MEM, kv_heads, group_size, HD)
    d_probs = exact_einsum('qgjd,kgd->gjqk', d_grid, v_grid)
    d_scores = read_probs * (d_probs - lax.optimization_barrier(jnp.sum(read_probs * d_probs, axis=-1, keepdims=True))) * HD ** (-0.5)
    d_scores = d_scores.astype(jnp.bfloat16)
    d_keys = exact_einsum('gjqk,qgjd->kgd', d_scores, q_grid)
    d_values = exact_einsum('gjqk,qgjd->kgd', read_weights, d_grid)
    return (d_keys.reshape(d_keys.shape[0], -1), d_values.reshape(d_values.shape[0], -1))

def normalize(memory_state):
    state_grid = memory_state.reshape(MEM, -1, HD)
    inv_rms = lax.rsqrt(lax.optimization_barrier(jnp.mean(state_grid * state_grid, axis=-1, keepdims=True)) + epsilon)
    return (state_grid * inv_rms, inv_rms)

def memory_tokens(normed):
    split_grid = normed.reshape(MEM, -1, 2, HD)
    mem_keys = split_grid[:, :, 0, :].reshape(MEM, -1).astype(jnp.bfloat16)
    mem_values = split_grid[:, :, 1, :].reshape(MEM, -1).astype(jnp.bfloat16)
    return (mem_keys, mem_values)

def normalize_back(memory_state, inv_rms, d_mem_keys, d_mem_values):
    kv_heads = d_mem_keys.shape[1] // HD
    d_grid = jnp.stack([d_mem_keys.reshape(MEM, kv_heads, HD), d_mem_values.reshape(MEM, kv_heads, HD)], axis=2)
    d_grid = d_grid.reshape(MEM, 2 * kv_heads, HD)
    state_grid = memory_state.reshape(MEM, -1, HD)
    d_state = inv_rms * d_grid - state_grid * inv_rms ** 3 * lax.optimization_barrier(jnp.mean(d_grid * state_grid, axis=-1, keepdims=True))
    return d_state.reshape(MEM, -1)

def segment_pass(seg_queries, keys_all, values_all, live_mask, seg_grad):
    row_count = seg_queries.shape[0]
    kv_heads = keys_all.shape[1] // HD
    group_size = seg_queries.shape[1] // HD // kv_heads
    q_grid = seg_queries.reshape(row_count, kv_heads, group_size, HD)
    k_grid = keys_all.reshape(-1, kv_heads, HD)
    v_grid = values_all.reshape(-1, kv_heads, HD)
    g_grid = seg_grad.reshape(row_count, kv_heads, group_size, HD)
    scores = exact_einsum('qgjd,kgd->gjqk', q_grid, k_grid) * HD ** (-0.5)
    scores = jnp.where(live_mask[None, None], scores, -1e+30)
    attn_probs = softmax_rows(scores)
    weights = attn_probs.astype(jnp.bfloat16)
    output = exact_einsum('gjqk,kgd->qgjd', weights, v_grid)
    d_probs = exact_einsum('qgjd,kgd->gjqk', g_grid, v_grid)
    d_scores = attn_probs * (d_probs - lax.optimization_barrier(jnp.sum(attn_probs * d_probs, axis=-1, keepdims=True))) * HD ** (-0.5)
    d_scores = d_scores.astype(jnp.bfloat16)
    d_queries = exact_einsum('gjqk,kgd->qgjd', d_scores, k_grid)
    d_keys = exact_einsum('gjqk,qgjd->kgd', d_scores, q_grid)
    d_values = exact_einsum('gjqk,qgjd->kgd', weights, g_grid)
    return (output.reshape(row_count, -1).astype(jnp.bfloat16), d_queries.reshape(row_count, -1).astype(jnp.bfloat16), d_keys.reshape(d_keys.shape[0], -1), d_values.reshape(d_values.shape[0], -1))

def reference(queries, keys, values, mem_queries, mem_proj, mem_decay, pattern, grad_out):
    q_seg = queries.reshape(SEGS, SEG, -1)
    k_seg = keys.reshape(SEGS, SEG, -1)
    v_seg = values.reshape(SEGS, SEG, -1)
    g_seg = grad_out.reshape(SEGS, SEG, -1)
    channels = mem_proj.shape[0]

    def write_one(inputs):
        summary = read_out(mem_queries, inputs[0], inputs[1])[0]
        return jnp.dot(summary, mem_proj.T, preferred_element_type=jnp.float32)
    writes = lax.map(write_one, (k_seg, v_seg))

    def forward_step(running, element):
        return (element[0][None, :] * running + element[1], running)
    _, states = lax.scan(forward_step, jnp.zeros((MEM, channels), jnp.float32), (mem_decay, writes))

    def attend_one(inputs):
        seg_queries, seg_keys, seg_values, seg_grad, tile_bits, memory_state = inputs
        normed, inv_rms = normalize(memory_state)
        mem_keys, mem_values = memory_tokens(normed)
        keys_all = jnp.concatenate([mem_keys, seg_keys], axis=0)
        values_all = jnp.concatenate([mem_values, seg_values], axis=0)
        live_mask = tile_mask(tile_bits, SEG)
        output, d_queries, d_keys, d_values = segment_pass(seg_queries, keys_all, values_all, live_mask, seg_grad)
        d_state = normalize_back(memory_state, inv_rms, d_keys[:MEM], d_values[:MEM])
        return (output, d_queries, d_keys[MEM:], d_values[MEM:], d_state)
    outputs, d_queries, d_keys, d_values, d_states = lax.map(attend_one, (q_seg, k_seg, v_seg, g_seg, pattern, states))

    def backward_step(running, element):
        return (element[1] + element[0][None, :] * running, running)
    _, d_writes = lax.scan(backward_step, jnp.zeros((MEM, channels), jnp.float32), (mem_decay, d_states), reverse=True)
    proj_wide = mem_proj.astype(jnp.float32)

    def write_back(inputs):
        seg_keys, seg_values, d_write = inputs
        summary, read_probs, read_weights = read_out(mem_queries, seg_keys, seg_values)
        d_summary = jnp.dot(d_write, proj_wide, precision=lax.Precision.HIGHEST).astype(jnp.bfloat16)
        return read_back(mem_queries, seg_keys, seg_values, read_probs, read_weights, d_summary)
    read_keys, read_values = lax.map(write_back, (k_seg, v_seg, d_writes))
    grad_keys = (d_keys + read_keys).astype(jnp.bfloat16).reshape(TOKENS, -1)
    grad_values = (d_values + read_values).astype(jnp.bfloat16).reshape(TOKENS, -1)
    return (outputs.reshape(TOKENS, -1), d_queries.reshape(TOKENS, -1), grad_keys, grad_values)
```

```python
import functools

import jax
import jax.numpy as jnp
from jax import lax
from jax.experimental import pallas as pl
from jax.experimental.pallas import tpu as pltpu
from jax.sharding import PartitionSpec as P

HD = 128
MEM = 128
BLOCK = 128
EPSILON = 1e-06
DEAD = -1e30
CHUNKS = 4
SCALE = HD ** (-0.5)
F32 = jnp.float32
BF16 = jnp.bfloat16

NN = (((1,), (0,)), ((), ()))
NT = (((1,), (1,)), ((), ()))
TN = (((0,), (0,)), ((), ()))


def dot(a, b, dims):
    return lax.dot_general(a, b, dims, preferred_element_type=F32)


def heads_loop(first, last, step, fn):
    if first >= last:
        return

    def lap(i, _):
        for j in range(step):
            fn(first + i * step + j)
        return 0

    lax.fori_loop(0, (last - first) // step, lap, 0)


def kernel(
    seqs, tensors,
    q_hbm, k_hbm, v_hbm, mq_hbm, mp_hbm, decay_ref, pattern_ref, do_hbm,
    o_hbm, gq_hbm, gk_ref, gv_ref,
    q_v, k_v, v_v, mq_v, mp_v, do_v, o_v, gq_v,
    rp_v, rw_v, sum_v, bias_v, mbias_v,
    p_v, dp_v, m_v, l_v, dd_v, pm_v, dsm_v, coef_v, row_v,
    core_send, core_recv, own_part, x_send, x_recv,
    dec_own, dec_peer, w_own, w_peer, e_send, e_recv,
    state_v, mk_v, mv_v, dmk_v, dmv_v, ds_own, ds_peer, b_send, b_recv,
    r_own, ag_x, ag_core, dsum_v, dk_v, dv_v,
    load_sem, store_sem,
    core_s, core_r, x_s, x_r, dec_s, dec_r, y_s, y_r, z_s, z_r,
    by_s, by_r, bz_s, bz_r, ax_s, ax_r, ac_s, ac_r,
):
    seg = k_v.shape[0]
    group = q_v.shape[1] // HD
    width = own_part.shape[2]
    rows = MEM // CHUNKS
    half_t, half_s = tensors // 2, seqs // 2
    si, ti = lax.axis_index("seq"), lax.axis_index("tensor")
    zi, yi = si // 2, si % 2
    xi, ci = ti // 2, ti % 2
    y = yi.astype(F32)
    n_y = 1.0 - y
    core_dev = {"seq": si, "tensor": xi * 2 + (1 - ci)}
    y_dev = {"seq": zi * 2 + (1 - yi), "tensor": ti}
    up_dev = {"seq": (si + 2) % seqs, "tensor": ti}
    down_dev = {"seq": (si + seqs - 2) % seqs, "tensor": ti}
    x_devs = [{"seq": si, "tensor": ((xi + 1 + n) % half_t) * 2 + ci} for n in range(half_t - 1)]
    has_down, has_up = zi > 0, zi < half_s - 1

    def remote(src, dst, send, recv, device):
        return pltpu.make_async_remote_copy(
            src_ref=src, dst_ref=dst, send_sem=send, recv_sem=recv,
            device_id=device, device_id_type=pl.DeviceIdType.MESH,
        )

    def head(h):
        return pl.ds(pl.multiple_of(h * HD, HD), HD)

    loads = [
        pltpu.make_async_copy(src, dst, load_sem.at[n])
        for n, (src, dst) in enumerate(
            ((k_hbm, k_v), (mq_hbm, mq_v), (v_hbm, v_v), (mp_hbm, mp_v), (q_hbm, q_v), (do_hbm, do_v))
        )
    ]
    for load in loads:
        load.start()
    barrier = pltpu.get_barrier_semaphore()

    def greet(device):
        pl.semaphore_signal(barrier, inc=1, device_id=device, device_id_type=pl.DeviceIdType.MESH)

    greet(core_dev)
    greet(y_dev)
    for device in x_devs:
        greet(device)

    @pl.when(has_down)
    def _():
        greet(down_dev)

    @pl.when(has_up)
    def _():
        greet(up_dev)

    dec_own[...] = jnp.broadcast_to(decay_ref[...], dec_own.shape)

    tiles = seg // BLOCK
    tile_row = lax.broadcasted_iota(jnp.int32, (BLOCK, BLOCK), 0)
    tile_col = lax.broadcasted_iota(jnp.int32, (BLOCK, BLOCK), 1)
    diagonal = jnp.where(tile_row <= tile_col, 0.0, DEAD)
    zero_tile = jnp.zeros((BLOCK, BLOCK), F32)
    for b in range(tiles):
        at_b = slice(b * BLOCK, (b + 1) * BLOCK)
        off = (1.0 - pattern_ref[0, b, 0].astype(F32)) * DEAD
        mbias_v[:, at_b] = jnp.zeros((8, BLOCK), F32) + off
        for j in range(tiles):
            at_j = slice(j * BLOCK, (j + 1) * BLOCK)
            if j > b:
                bias_v[at_j, at_b] = zero_tile + DEAD
            else:
                off = (1.0 - pattern_ref[0, b, 1 + j].astype(F32)) * DEAD
                bias_v[at_j, at_b] = (diagonal if j == b else zero_tile) + off

    for load in loads[:3]:
        load.wait()

    def read_head(h):
        scores = dot(k_v[...], mq_v[:, head(h)], NT) * SCALE
        raised = jnp.exp(scores - jnp.max(scores, axis=0, keepdims=True))
        probs = raised / jnp.sum(raised, axis=0, keepdims=True)
        rp_v[h] = probs
        weights = probs.astype(BF16)
        rw_v[h] = weights
        sum_v[:, head(h)] = dot(weights, v_v[...], TN).astype(BF16)

    heads_loop(0, group, 4, read_head)
    loads[3].wait()

    def proj_rows(block):
        return mp_v[pl.ds(pl.multiple_of(block * width, width), width), :]

    chained = jnp.minimum(zi, 1) + jnp.minimum(half_s - 1 - zi, 1)
    pl.semaphore_wait(barrier, 2 + len(x_devs) + chained)

    sent = []
    up_sent = []
    down_sent = []

    def send(*args):
        copy = remote(*args)
        copy.start()
        sent.append(copy)

    send(dec_own, dec_peer, dec_s.at[0], dec_r.at[0], y_dev)

    for n in range(half_t):
        there = (xi + 1 + n) % half_t
        core_send[n] = dot(sum_v[...], proj_rows(there * 2 + (1 - ci)), NT)
        send(core_send.at[n], core_recv.at[n], core_s.at[n], core_r.at[n], core_dev)
    for n in range(half_t):
        there = (xi + 1 + n) % half_t
        own_part[n] = dot(sum_v[...], proj_rows(there * 2 + ci), NT)
    for n in range(half_t - 1):
        remote(core_send.at[n], core_recv.at[n], core_s.at[n], core_r.at[n], core_dev).wait_recv()
        for c in range(CHUNKS):
            at = slice(c * rows, (c + 1) * rows)
            x_send[n, c] = own_part[n, at, :] + core_recv[n, at, :]
            send(x_send.at[n, c], x_recv.at[n, c], x_s.at[n, c], x_r.at[n, c], x_devs[n])

    loads[4].wait()
    loads[5].wait()

    def own_head(h):
        scores = dot(k_v[...], q_v[:, head(h)], NT) * SCALE + bias_v[...]
        top = jnp.max(scores, axis=0, keepdims=True)
        raised = jnp.exp(scores - top)
        d_probs = dot(v_v[...], do_v[:, head(h)], NT)
        p_v[h] = raised
        dp_v[h] = d_probs
        m_v[h] = top
        l_v[h] = jnp.sum(raised, axis=0, keepdims=True)
        dd_v[h] = jnp.sum(raised * d_probs, axis=0, keepdims=True)

    heads_loop(0, group // 2, 2, own_head)

    last = half_t - 1
    remote(core_send.at[last], core_recv.at[last], core_s.at[last], core_r.at[last], core_dev).wait_recv()
    for c in range(CHUNKS):
        at = slice(c * rows, (c + 1) * rows)
        total = own_part[last, at, :] + core_recv[last, at, :]
        for n in range(half_t - 1):
            remote(x_send.at[n, c], x_recv.at[n, c], x_s.at[n, c], x_r.at[n, c], x_devs[n]).wait_recv()
            total = total + x_recv[n, c]
        w_own[c] = total
        send(w_own.at[c], w_peer.at[c], y_s.at[c], y_r.at[c], y_dev)

    heads_loop(group // 2, group, 2, own_head)

    remote(dec_own, dec_peer, dec_s.at[0], dec_r.at[0], y_dev).wait_recv()
    mine = dec_own[0:1, :]
    peer = dec_peer[0:1, :]
    both = mine * peer

    @pl.when(zi == 0)
    def _():
        e_recv[...] = jnp.zeros_like(e_recv)

    for c in range(CHUNKS):
        at = slice(c * rows, (c + 1) * rows)
        remote(w_own.at[c], w_peer.at[c], y_s.at[c], y_r.at[c], y_dev).wait_recv()
        from_peer = w_peer[c]
        pair = (n_y * peer + y) * w_own[c] + (n_y + y * mine) * from_peer
        chain = remote(e_send.at[c], e_recv.at[c], z_s.at[c], z_r.at[c], up_dev)

        @pl.when(has_down)
        def _():
            chain.wait_recv()

        entering = e_recv[c]
        e_send[c] = both * entering + pair

        @pl.when(has_up)
        def _():
            chain.start()

        up_sent.append(chain)
        state = (n_y + y * peer) * entering + y * from_peer
        state_v[at, :] = state
        for part, out in ((0, mk_v), (1, mv_v)):
            grid = state[:, part * HD : (part + 1) * HD]
            inv = lax.rsqrt(jnp.mean(grid * grid, axis=-1, keepdims=True) + EPSILON)
            out[at, :] = (grid * inv).astype(BF16)

    dmk_v[...] = jnp.zeros_like(dmk_v)
    dmv_v[...] = jnp.zeros_like(dmv_v)

    def memory_head(h):
        q_h, do_h = q_v[:, head(h)], do_v[:, head(h)]
        scores = dot(mk_v[...], q_h, NT) * SCALE + mbias_v[0:1, :]
        own_top = m_v[h]
        top = jnp.maximum(own_top, jnp.max(scores, axis=0, keepdims=True))
        shrink = jnp.exp(own_top - top)
        raised = jnp.exp(scores - top)
        inv = 1.0 / (shrink * l_v[h] + jnp.sum(raised, axis=0, keepdims=True))
        probs = raised * inv
        coef = shrink * inv
        d_probs = dot(mv_v[...], do_h, NT)
        row = coef * dd_v[h] + jnp.sum(probs * d_probs, axis=0, keepdims=True)
        d_scores = (probs * (d_probs - row) * SCALE).astype(BF16)
        weights = probs.astype(BF16)
        pm_v[h] = weights
        dsm_v[h] = d_scores
        coef_v[h] = coef
        row_v[h] = row
        dmk_v[...] += dot(d_scores, q_h, NN)
        dmv_v[...] += dot(weights, do_h, NN)

    heads_loop(0, group, 4, memory_head)

    d_state = []
    for part, grad in ((0, dmk_v), (1, dmv_v)):
        grid = state_v[:, part * HD : (part + 1) * HD]
        inv = lax.rsqrt(jnp.mean(grid * grid, axis=-1, keepdims=True) + EPSILON)
        d_normed = grad[...]
        mean = jnp.mean(d_normed * grid, axis=-1, keepdims=True)
        d_state.append(inv * d_normed - grid * (inv * inv * inv * mean))
    for c in range(CHUNKS):
        at = slice(c * rows, (c + 1) * rows)
        for part in range(2):
            ds_own[c, :, part * HD : (part + 1) * HD] = d_state[part][at, :]
        send(ds_own.at[c], ds_peer.at[c], by_s.at[c], by_r.at[c], y_dev)

    dk_v[...] = jnp.zeros_like(dk_v)
    dv_v[...] = jnp.zeros_like(dv_v)

    def grad_head(h):
        q_h, do_h = q_v[:, head(h)], do_v[:, head(h)]
        probs = p_v[h] * coef_v[h]
        d_scores = (probs * (dp_v[h] - row_v[h]) * SCALE).astype(BF16)
        weights = probs.astype(BF16)
        o_v[:, head(h)] = (dot(weights, v_v[...], TN) + dot(pm_v[h], mv_v[...], TN)).astype(BF16)
        gq_v[:, head(h)] = (dot(d_scores, k_v[...], TN) + dot(dsm_v[h], mk_v[...], TN)).astype(BF16)
        dk_v[...] += dot(d_scores, q_h, NN)
        dv_v[...] += dot(weights, do_h, NN)

    heads_loop(0, group // 2, 2, grad_head)

    @pl.when(zi == half_s - 1)
    def _():
        b_recv[...] = jnp.zeros_like(b_recv)

    for c in range(CHUNKS):
        remote(ds_own.at[c], ds_peer.at[c], by_s.at[c], by_r.at[c], y_dev).wait_recv()
        from_peer = ds_peer[c]
        pair = (y * peer + n_y) * ds_own[c] + (n_y * mine + y) * from_peer
        chain = remote(b_send.at[c], b_recv.at[c], bz_s.at[c], bz_r.at[c], down_dev)

        @pl.when(has_up)
        def _():
            chain.wait_recv()

        entering = b_recv[c]
        b_send[c] = pair + both * entering

        @pl.when(has_down)
        def _():
            chain.start()

        down_sent.append(chain)
        at = slice(c * rows, (c + 1) * rows)
        r_own[at, :] = (y + n_y * peer) * entering + n_y * from_peer
        for n in range(half_t - 1):
            send(r_own.at[pl.ds(c * rows, rows)], ag_x.at[n, pl.ds(c * rows, rows)], ax_s.at[n, c], ax_r.at[n, c], x_devs[n])
        send(r_own.at[pl.ds(c * rows, rows)], ag_core.at[0, pl.ds(c * rows, rows)], ac_s.at[0, c], ac_r.at[0, c], core_dev)

    heads_loop(group // 2, group, 2, grad_head)
    stores = [
        pltpu.make_async_copy(o_v, o_hbm, store_sem.at[0]),
        pltpu.make_async_copy(gq_v, gq_hbm, store_sem.at[1]),
    ]
    for store in stores:
        store.start()

    def back(part, block):
        high = part.astype(BF16)
        low = (part - high.astype(F32)).astype(BF16)
        proj = proj_rows(block)
        return dot(high, proj, NN) + dot(low, proj, NN)

    total = back(r_own[...], ti)
    for n in range(half_t - 1):
        for c in range(CHUNKS):
            at = pl.ds(c * rows, rows)
            remote(r_own.at[at], ag_x.at[n, at], ax_s.at[n, c], ax_r.at[n, c], x_devs[n]).wait_recv()
            send(ag_x.at[n, at], ag_core.at[1 + n, at], ac_s.at[1 + n, c], ac_r.at[1 + n, c], core_dev)
    for n in range(half_t):
        for c in range(CHUNKS):
            at = pl.ds(c * rows, rows)
            remote(r_own.at[at], ag_core.at[n, at], ac_s.at[n, c], ac_r.at[n, c], core_dev).wait_recv()
        block = (xi + half_t - n) % half_t
        total = total + back(ag_core[n], block * 2 + (1 - ci))
        if n > 0:
            total = total + back(ag_x[n - 1], block * 2 + ci)
    dsum_v[...] = total.astype(BF16)

    def back_head(h):
        d_sum = dsum_v[:, head(h)]
        probs = rp_v[h]
        d_probs = dot(v_v[...], d_sum, NT)
        d_scores = probs * (d_probs - jnp.sum(probs * d_probs, axis=0, keepdims=True)) * SCALE
        dk_v[...] += dot(d_scores.astype(BF16), mq_v[:, head(h)], NN)
        dv_v[...] += dot(rw_v[h], d_sum, NN)

    heads_loop(0, group, 4, back_head)
    gk_ref[...] = dk_v[...].astype(BF16)
    gv_ref[...] = dv_v[...].astype(BF16)

    for copy in sent:
        copy.wait_send()
    for copy in up_sent:
        @pl.when(has_up)
        def _():
            copy.wait_send()
    for copy in down_sent:
        @pl.when(has_down)
        def _():
            copy.wait_send()
    for store in stores:
        store.wait()


def local(seqs, tensors, queries, keys, values, mem_queries, mem_proj, mem_decay, pattern, grad_out):
    seg, cols = queries.shape
    width = mem_decay.shape[1]
    group = cols // HD
    half_t = tensors // 2
    rows = MEM // CHUNKS
    assert keys.shape[1] == HD and width == 2 * HD
    assert seqs % 2 == 0 and tensors % 2 == 0
    vmem = pl.BlockSpec(memory_space=pltpu.VMEM)
    anywhere = pl.BlockSpec(memory_space=pl.ANY)
    like = lambda a: pltpu.VMEM(a.shape, a.dtype)
    f32 = lambda *shape: pltpu.VMEM(shape, F32)
    b16 = lambda *shape: pltpu.VMEM(shape, BF16)
    dma = lambda *shape: pltpu.SemaphoreType.DMA(shape)
    chunk = f32(CHUNKS, rows, width)
    return pl.pallas_call(
        functools.partial(kernel, seqs, tensors),
        out_shape=tuple(jax.ShapeDtypeStruct(a.shape, BF16) for a in (grad_out, queries, keys, values)),
        in_specs=[
            anywhere, anywhere, anywhere, anywhere, anywhere, vmem,
            pl.BlockSpec(memory_space=pltpu.SMEM), anywhere,
        ],
        out_specs=(anywhere, anywhere, vmem, vmem),
        scratch_shapes=[
            like(queries), like(keys), like(values), like(mem_queries), like(mem_proj),
            like(grad_out), like(grad_out), like(queries),
            f32(group, seg, MEM), b16(group, seg, MEM), like(mem_queries), f32(seg, seg), f32(8, seg),
            f32(group, seg, seg), f32(group, seg, seg),
            f32(group, 1, seg), f32(group, 1, seg), f32(group, 1, seg),
            b16(group, MEM, seg), b16(group, MEM, seg), f32(group, 1, seg), f32(group, 1, seg),
            f32(half_t, MEM, width), f32(half_t, MEM, width), f32(half_t, MEM, width),
            f32(max(half_t - 1, 1), CHUNKS, rows, width), f32(max(half_t - 1, 1), CHUNKS, rows, width),
            f32(8, width), f32(8, width), chunk, chunk, chunk, chunk,
            f32(MEM, width), b16(MEM, HD), b16(MEM, HD), f32(MEM, HD), f32(MEM, HD),
            chunk, chunk, chunk, chunk,
            f32(MEM, width), f32(max(half_t - 1, 1), MEM, width), f32(half_t, MEM, width),
            like(mem_queries), f32(seg, HD), f32(seg, HD),
            dma(6), dma(2),
            dma(half_t), dma(half_t),
            dma(max(half_t - 1, 1), CHUNKS), dma(max(half_t - 1, 1), CHUNKS),
            dma(1), dma(1), dma(CHUNKS), dma(CHUNKS), dma(CHUNKS), dma(CHUNKS),
            dma(CHUNKS), dma(CHUNKS), dma(CHUNKS), dma(CHUNKS),
            dma(max(half_t - 1, 1), CHUNKS), dma(max(half_t - 1, 1), CHUNKS),
            dma(half_t, CHUNKS), dma(half_t, CHUNKS),
        ],
        compiler_params=pltpu.CompilerParams(collective_id=0, has_side_effects=True),
    )(queries, keys, values, mem_queries, mem_proj, mem_decay, pattern, grad_out)


def solution(mesh):
    cut = P("seq", "tensor")
    placed = (cut, cut, cut, P(None, "tensor"), P(None, "tensor"), cut, P("seq", None, None), cut)
    return jax.shard_map(
        functools.partial(local, mesh.shape["seq"], mesh.shape["tensor"]),
        mesh=mesh,
        in_specs=placed,
        out_specs=(cut, cut, cut, cut),
        check_vma=False,
    )
```

```python
import functools

import jax
import jax.numpy as jnp
from jax import lax
from jax.experimental import pallas as pl
from jax.experimental.pallas import tpu as pltpu
from jax.sharding import PartitionSpec as P

HD = 128
MEM = 128
BLOCK = 128
EPSILON = 1e-06
DEAD = -1e30
CHUNKS = 4
SCALE = HD ** (-0.5)
F32 = jnp.float32
BF16 = jnp.bfloat16

NN = (((1,), (0,)), ((), ()))
NT = (((1,), (1,)), ((), ()))
TN = (((0,), (0,)), ((), ()))


def dot(a, b, dims):
    return lax.dot_general(a, b, dims, preferred_element_type=F32)


def heads_loop(first, last, step, fn):
    if first >= last:
        return

    def lap(i, _):
        for j in range(step):
            fn(first + i * step + j)
        return 0

    lax.fori_loop(0, (last - first) // step, lap, 0)


def kernel(
    seqs, tensors,
    q_hbm, k_hbm, v_hbm, mq_hbm, mp_hbm, decay_ref, pattern_ref, do_hbm,
    o_hbm, gq_hbm, gk_ref, gv_ref,
    q_v, k_v, v_v, mq_v, mp_v, do_v, o_v, gq_v,
    rp_v, rw_v, sum_v, bias_v, mbias_v,
    p_v, dp_v, m_v, l_v, dd_v, pm_v, dsm_v, coef_v, row_v,
    core_send, core_recv, own_part, x_send, x_recv,
    dec_own, dec_peer, w_own, w_peer, e_send, e_recv,
    state_v, mk_v, mv_v, dmk_v, dmv_v, ds_own, ds_peer, b_send, b_recv,
    r_own, ag_x, ag_core, dsum_v, dk_v, dv_v,
    load_sem, store_sem,
    core_s, core_r, x_s, x_r, dec_s, dec_r, y_s, y_r, z_s, z_r,
    by_s, by_r, bz_s, bz_r, ax_s, ax_r, ac_s, ac_r,
):
    seg = k_v.shape[0]
    group = q_v.shape[1] // HD
    width = own_part.shape[2]
    rows = MEM // CHUNKS
    half_t, groups = tensors // 2, seqs // 4
    si, ti = lax.axis_index("seq"), lax.axis_index("tensor")
    gi, ri, yi = si // 4, (si // 2) % 2, si % 2
    xi, ci = ti // 2, ti % 2
    y, r = yi.astype(F32), ri.astype(F32)
    n_y, n_r = 1.0 - y, 1.0 - r
    core_dev = {"seq": si, "tensor": xi * 2 + (1 - ci)}
    y_dev = {"seq": gi * 4 + ri * 2 + (1 - yi), "tensor": ti}
    row_devs = [{"seq": gi * 4 + (1 - ri) * 2 + where, "tensor": ti} for where in (yi, 1 - yi)]
    group_devs = [y_dev] + row_devs
    after, before = (gi + 1) % groups, (gi + groups - 1) % groups
    up_devs = [{"seq": after * 4 + row * 2 + yi, "tensor": ti} for row in (1, 0)]
    down_devs = [{"seq": before * 4 + row * 2 + yi, "tensor": ti} for row in (0, 1)]
    x_devs = [{"seq": si, "tensor": ((xi + 1 + n) % half_t) * 2 + ci} for n in range(half_t - 1)]
    has_down, has_up = gi > 0, gi < groups - 1
    sends_up, sends_down = has_up & (ri == 1), has_down & (ri == 0)

    def remote(src, dst, send, recv, device):
        return pltpu.make_async_remote_copy(
            src_ref=src, dst_ref=dst, send_sem=send, recv_sem=recv,
            device_id=device, device_id_type=pl.DeviceIdType.MESH,
        )

    def head(h):
        return pl.ds(pl.multiple_of(h * HD, HD), HD)

    loads = [
        pltpu.make_async_copy(src, dst, load_sem.at[n])
        for n, (src, dst) in enumerate(
            ((k_hbm, k_v), (mq_hbm, mq_v), (v_hbm, v_v), (mp_hbm, mp_v), (q_hbm, q_v), (do_hbm, do_v))
        )
    ]
    for load in loads:
        load.start()
    barrier = pltpu.get_barrier_semaphore()

    def greet(device):
        pl.semaphore_signal(barrier, inc=1, device_id=device, device_id_type=pl.DeviceIdType.MESH)

    greet(core_dev)
    for device in group_devs + x_devs:
        greet(device)

    @pl.when(has_down)
    def _():
        greet(down_devs[1])

    @pl.when(has_up)
    def _():
        greet(up_devs[1])

    dec_own[...] = jnp.broadcast_to(decay_ref[...], dec_own.shape)

    tiles = seg // BLOCK
    tile_row = lax.broadcasted_iota(jnp.int32, (BLOCK, BLOCK), 0)
    tile_col = lax.broadcasted_iota(jnp.int32, (BLOCK, BLOCK), 1)
    diagonal = jnp.where(tile_row <= tile_col, 0.0, DEAD)
    zero_tile = jnp.zeros((BLOCK, BLOCK), F32)
    for b in range(tiles):
        at_b = slice(b * BLOCK, (b + 1) * BLOCK)
        off = (1.0 - pattern_ref[0, b, 0].astype(F32)) * DEAD
        mbias_v[:, at_b] = jnp.zeros((8, BLOCK), F32) + off
        for j in range(tiles):
            at_j = slice(j * BLOCK, (j + 1) * BLOCK)
            if j > b:
                bias_v[at_j, at_b] = zero_tile + DEAD
            else:
                off = (1.0 - pattern_ref[0, b, 1 + j].astype(F32)) * DEAD
                bias_v[at_j, at_b] = (diagonal if j == b else zero_tile) + off

    for load in loads[:3]:
        load.wait()

    def read_head(h):
        scores = dot(k_v[...], mq_v[:, head(h)], NT) * SCALE
        raised = jnp.exp(scores - jnp.max(scores, axis=0, keepdims=True))
        probs = raised / jnp.sum(raised, axis=0, keepdims=True)
        rp_v[h] = probs
        weights = probs.astype(BF16)
        rw_v[h] = weights
        sum_v[:, head(h)] = dot(weights, v_v[...], TN).astype(BF16)

    heads_loop(0, group, 4, read_head)
    loads[3].wait()

    def proj_rows(block):
        return mp_v[pl.ds(pl.multiple_of(block * width, width), width), :]

    chained = 2 * (ri * jnp.minimum(groups - 1 - gi, 1) + (1 - ri) * jnp.minimum(gi, 1))
    pl.semaphore_wait(barrier, 1 + len(group_devs) + len(x_devs) + chained)

    sent = []
    row_sent = []
    row_back = []
    up_sent = []
    down_sent = []

    def send(*args):
        copy = remote(*args)
        copy.start()
        sent.append(copy)

    def row_pair(own, peers, send_sems, recv_sems, c):
        return [
            remote(own.at[c], peers.at[1 + n, c], send_sems.at[1 + n, c], recv_sems.at[1 + n, c], row_devs[n])
            for n in range(2)
        ]

    for n, device in enumerate(group_devs):
        send(dec_own, dec_peer.at[n], dec_s.at[n], dec_r.at[n], device)

    for n in range(half_t):
        there = (xi + 1 + n) % half_t
        core_send[n] = dot(sum_v[...], proj_rows(there * 2 + (1 - ci)), NT)
        send(core_send.at[n], core_recv.at[n], core_s.at[n], core_r.at[n], core_dev)
    for n in range(half_t):
        there = (xi + 1 + n) % half_t
        own_part[n] = dot(sum_v[...], proj_rows(there * 2 + ci), NT)
    for n in range(half_t - 1):
        remote(core_send.at[n], core_recv.at[n], core_s.at[n], core_r.at[n], core_dev).wait_recv()
        for c in range(CHUNKS):
            at = slice(c * rows, (c + 1) * rows)
            x_send[n, c] = own_part[n, at, :] + core_recv[n, at, :]
            send(x_send.at[n, c], x_recv.at[n, c], x_s.at[n, c], x_r.at[n, c], x_devs[n])

    loads[4].wait()
    loads[5].wait()

    def own_head(h):
        scores = dot(k_v[...], q_v[:, head(h)], NT) * SCALE + bias_v[...]
        top = jnp.max(scores, axis=0, keepdims=True)
        raised = jnp.exp(scores - top)
        d_probs = dot(v_v[...], do_v[:, head(h)], NT)
        p_v[h] = raised
        dp_v[h] = d_probs
        m_v[h] = top
        l_v[h] = jnp.sum(raised, axis=0, keepdims=True)
        dd_v[h] = jnp.sum(raised * d_probs, axis=0, keepdims=True)

    heads_loop(0, group // 2, 2, own_head)

    last = half_t - 1
    remote(core_send.at[last], core_recv.at[last], core_s.at[last], core_r.at[last], core_dev).wait_recv()
    for c in range(CHUNKS):
        at = slice(c * rows, (c + 1) * rows)
        total = own_part[last, at, :] + core_recv[last, at, :]
        for n in range(half_t - 1):
            remote(x_send.at[n, c], x_recv.at[n, c], x_s.at[n, c], x_r.at[n, c], x_devs[n]).wait_recv()
            total = total + x_recv[n, c]
        w_own[c] = total
        send(w_own.at[c], w_peer.at[0, c], y_s.at[0, c], y_r.at[0, c], y_dev)
        row_copies = row_pair(w_own, w_peer, y_s, y_r, c)

        @pl.when(ri == 0)
        def _():
            for copy in row_copies:
                copy.start()

        row_sent.extend(row_copies)

    heads_loop(group // 2, group, 2, own_head)

    for n, device in enumerate(group_devs):
        remote(dec_own, dec_peer.at[n], dec_s.at[n], dec_r.at[n], device).wait_recv()
    mine, peer, same, cross = dec_own[0:1, :], dec_peer[0, 0:1, :], dec_peer[1, 0:1, :], dec_peer[2, 0:1, :]
    both, other = mine * peer, same * cross

    @pl.when(gi == 0)
    def _():
        e_recv[...] = jnp.zeros_like(e_recv)

    @pl.when(ri == 0)
    def _():
        w_peer[1] = jnp.zeros(w_peer.shape[1:], F32)
        w_peer[2] = jnp.zeros(w_peer.shape[1:], F32)

    for c in range(CHUNKS):
        at = slice(c * rows, (c + 1) * rows)
        remote(w_own.at[c], w_peer.at[0, c], y_s.at[0, c], y_r.at[0, c], y_dev).wait_recv()
        row_copies = row_pair(w_own, w_peer, y_s, y_r, c)

        @pl.when(ri == 1)
        def _():
            for copy in row_copies:
                copy.wait_recv()

        from_peer = w_peer[0, c]
        pair = (n_y * peer + y) * w_own[c] + (n_y + y * mine) * from_peer
        earlier = (n_y * cross + y) * w_peer[1, c] + (n_y + y * same) * w_peer[2, c]
        chain = [remote(e_send.at[c], e_recv.at[c], z_s.at[n, c], z_r.at[c], up_devs[n]) for n in range(2)]

        @pl.when(has_down)
        def _():
            chain[0].wait_recv()

        entering = (n_r + r * other) * e_recv[c] + r * earlier
        e_send[c] = both * entering + pair

        @pl.when(sends_up)
        def _():
            for copy in chain:
                copy.start()

        up_sent.extend(chain)
        state = (n_y + y * peer) * entering + y * from_peer
        state_v[at, :] = state
        for part, out in ((0, mk_v), (1, mv_v)):
            grid = state[:, part * HD : (part + 1) * HD]
            inv = lax.rsqrt(jnp.mean(grid * grid, axis=-1, keepdims=True) + EPSILON)
            out[at, :] = (grid * inv).astype(BF16)

    dmk_v[...] = jnp.zeros_like(dmk_v)
    dmv_v[...] = jnp.zeros_like(dmv_v)

    def memory_head(h):
        q_h, do_h = q_v[:, head(h)], do_v[:, head(h)]
        scores = dot(mk_v[...], q_h, NT) * SCALE + mbias_v[0:1, :]
        own_top = m_v[h]
        top = jnp.maximum(own_top, jnp.max(scores, axis=0, keepdims=True))
        shrink = jnp.exp(own_top - top)
        raised = jnp.exp(scores - top)
        inv = 1.0 / (shrink * l_v[h] + jnp.sum(raised, axis=0, keepdims=True))
        probs = raised * inv
        coef = shrink * inv
        d_probs = dot(mv_v[...], do_h, NT)
        row = coef * dd_v[h] + jnp.sum(probs * d_probs, axis=0, keepdims=True)
        d_scores = (probs * (d_probs - row) * SCALE).astype(BF16)
        weights = probs.astype(BF16)
        pm_v[h] = weights
        dsm_v[h] = d_scores
        coef_v[h] = coef
        row_v[h] = row
        dmk_v[...] += dot(d_scores, q_h, NN)
        dmv_v[...] += dot(weights, do_h, NN)

    heads_loop(0, group, 4, memory_head)

    d_state = []
    for part, grad in ((0, dmk_v), (1, dmv_v)):
        grid = state_v[:, part * HD : (part + 1) * HD]
        inv = lax.rsqrt(jnp.mean(grid * grid, axis=-1, keepdims=True) + EPSILON)
        d_normed = grad[...]
        mean = jnp.mean(d_normed * grid, axis=-1, keepdims=True)
        d_state.append(inv * d_normed - grid * (inv * inv * inv * mean))
    for c in range(CHUNKS):
        at = slice(c * rows, (c + 1) * rows)
        for part in range(2):
            ds_own[c, :, part * HD : (part + 1) * HD] = d_state[part][at, :]
        send(ds_own.at[c], ds_peer.at[0, c], by_s.at[0, c], by_r.at[0, c], y_dev)
        row_copies = row_pair(ds_own, ds_peer, by_s, by_r, c)

        @pl.when(ri == 1)
        def _():
            for copy in row_copies:
                copy.start()

        row_back.extend(row_copies)

    dk_v[...] = jnp.zeros_like(dk_v)
    dv_v[...] = jnp.zeros_like(dv_v)

    def grad_head(h):
        q_h, do_h = q_v[:, head(h)], do_v[:, head(h)]
        probs = p_v[h] * coef_v[h]
        d_scores = (probs * (dp_v[h] - row_v[h]) * SCALE).astype(BF16)
        weights = probs.astype(BF16)
        o_v[:, head(h)] = (dot(weights, v_v[...], TN) + dot(pm_v[h], mv_v[...], TN)).astype(BF16)
        gq_v[:, head(h)] = (dot(d_scores, k_v[...], TN) + dot(dsm_v[h], mk_v[...], TN)).astype(BF16)
        dk_v[...] += dot(d_scores, q_h, NN)
        dv_v[...] += dot(weights, do_h, NN)

    heads_loop(0, group // 2, 2, grad_head)

    @pl.when(gi == groups - 1)
    def _():
        b_recv[...] = jnp.zeros_like(b_recv)

    @pl.when(ri == 1)
    def _():
        ds_peer[1] = jnp.zeros(ds_peer.shape[1:], F32)
        ds_peer[2] = jnp.zeros(ds_peer.shape[1:], F32)

    for c in range(CHUNKS):
        remote(ds_own.at[c], ds_peer.at[0, c], by_s.at[0, c], by_r.at[0, c], y_dev).wait_recv()
        row_copies = row_pair(ds_own, ds_peer, by_s, by_r, c)

        @pl.when(ri == 0)
        def _():
            for copy in row_copies:
                copy.wait_recv()

        from_peer = ds_peer[0, c]
        pair = (y * peer + n_y) * ds_own[c] + (n_y * mine + y) * from_peer
        later = (y * cross + n_y) * ds_peer[1, c] + (n_y * same + y) * ds_peer[2, c]
        chain = [remote(b_send.at[c], b_recv.at[c], bz_s.at[n, c], bz_r.at[c], down_devs[n]) for n in range(2)]

        @pl.when(has_up)
        def _():
            chain[0].wait_recv()

        entering = (r + n_r * other) * b_recv[c] + n_r * later
        b_send[c] = pair + both * entering

        @pl.when(sends_down)
        def _():
            for copy in chain:
                copy.start()

        down_sent.extend(chain)
        at = slice(c * rows, (c + 1) * rows)
        r_own[at, :] = (y + n_y * peer) * entering + n_y * from_peer
        for n in range(half_t - 1):
            send(r_own.at[pl.ds(c * rows, rows)], ag_x.at[n, pl.ds(c * rows, rows)], ax_s.at[n, c], ax_r.at[n, c], x_devs[n])
        send(r_own.at[pl.ds(c * rows, rows)], ag_core.at[0, pl.ds(c * rows, rows)], ac_s.at[0, c], ac_r.at[0, c], core_dev)

    heads_loop(group // 2, group, 2, grad_head)
    stores = [
        pltpu.make_async_copy(o_v, o_hbm, store_sem.at[0]),
        pltpu.make_async_copy(gq_v, gq_hbm, store_sem.at[1]),
    ]
    for store in stores:
        store.start()

    def back(part, block):
        high = part.astype(BF16)
        low = (part - high.astype(F32)).astype(BF16)
        proj = proj_rows(block)
        return dot(high, proj, NN) + dot(low, proj, NN)

    total = back(r_own[...], ti)
    for n in range(half_t - 1):
        for c in range(CHUNKS):
            at = pl.ds(c * rows, rows)
            remote(r_own.at[at], ag_x.at[n, at], ax_s.at[n, c], ax_r.at[n, c], x_devs[n]).wait_recv()
            send(ag_x.at[n, at], ag_core.at[1 + n, at], ac_s.at[1 + n, c], ac_r.at[1 + n, c], core_dev)
    for n in range(half_t):
        for c in range(CHUNKS):
            at = pl.ds(c * rows, rows)
            remote(r_own.at[at], ag_core.at[n, at], ac_s.at[n, c], ac_r.at[n, c], core_dev).wait_recv()
        block = (xi + half_t - n) % half_t
        total = total + back(ag_core[n], block * 2 + (1 - ci))
        if n > 0:
            total = total + back(ag_x[n - 1], block * 2 + ci)
    dsum_v[...] = total.astype(BF16)

    def back_head(h):
        d_sum = dsum_v[:, head(h)]
        probs = rp_v[h]
        d_probs = dot(v_v[...], d_sum, NT)
        d_scores = probs * (d_probs - jnp.sum(probs * d_probs, axis=0, keepdims=True)) * SCALE
        dk_v[...] += dot(d_scores.astype(BF16), mq_v[:, head(h)], NN)
        dv_v[...] += dot(rw_v[h], d_sum, NN)

    heads_loop(0, group, 4, back_head)
    gk_ref[...] = dk_v[...].astype(BF16)
    gv_ref[...] = dv_v[...].astype(BF16)

    for copy in sent:
        copy.wait_send()
    for ends, copies in (
        (sends_up, up_sent), (sends_down, down_sent), (ri == 0, row_sent), (ri == 1, row_back)
    ):
        @pl.when(ends)
        def _():
            for copy in copies:
                copy.wait_send()

    for store in stores:
        store.wait()


def local(seqs, tensors, queries, keys, values, mem_queries, mem_proj, mem_decay, pattern, grad_out):
    seg, cols = queries.shape
    width = mem_decay.shape[1]
    group = cols // HD
    half_t = tensors // 2
    rows = MEM // CHUNKS
    assert keys.shape[1] == HD and width == 2 * HD
    assert seqs % 4 == 0 and tensors % 2 == 0
    vmem = pl.BlockSpec(memory_space=pltpu.VMEM)
    anywhere = pl.BlockSpec(memory_space=pl.ANY)
    like = lambda a: pltpu.VMEM(a.shape, a.dtype)
    f32 = lambda *shape: pltpu.VMEM(shape, F32)
    b16 = lambda *shape: pltpu.VMEM(shape, BF16)
    dma = lambda *shape: pltpu.SemaphoreType.DMA(shape)
    chunk = f32(CHUNKS, rows, width)
    chunks3 = f32(3, CHUNKS, rows, width)
    return pl.pallas_call(
        functools.partial(kernel, seqs, tensors),
        out_shape=tuple(jax.ShapeDtypeStruct(a.shape, BF16) for a in (grad_out, queries, keys, values)),
        in_specs=[
            anywhere, anywhere, anywhere, anywhere, anywhere, vmem,
            pl.BlockSpec(memory_space=pltpu.SMEM), anywhere,
        ],
        out_specs=(anywhere, anywhere, vmem, vmem),
        scratch_shapes=[
            like(queries), like(keys), like(values), like(mem_queries), like(mem_proj),
            like(grad_out), like(grad_out), like(queries),
            f32(group, seg, MEM), b16(group, seg, MEM), like(mem_queries), f32(seg, seg), f32(8, seg),
            f32(group, seg, seg), f32(group, seg, seg),
            f32(group, 1, seg), f32(group, 1, seg), f32(group, 1, seg),
            b16(group, MEM, seg), b16(group, MEM, seg), f32(group, 1, seg), f32(group, 1, seg),
            f32(half_t, MEM, width), f32(half_t, MEM, width), f32(half_t, MEM, width),
            f32(max(half_t - 1, 1), CHUNKS, rows, width), f32(max(half_t - 1, 1), CHUNKS, rows, width),
            f32(8, width), f32(3, 8, width), chunk, chunks3, chunk, chunk,
            f32(MEM, width), b16(MEM, HD), b16(MEM, HD), f32(MEM, HD), f32(MEM, HD),
            chunk, chunks3, chunk, chunk,
            f32(MEM, width), f32(max(half_t - 1, 1), MEM, width), f32(half_t, MEM, width),
            like(mem_queries), f32(seg, HD), f32(seg, HD),
            dma(6), dma(2),
            dma(half_t), dma(half_t),
            dma(max(half_t - 1, 1), CHUNKS), dma(max(half_t - 1, 1), CHUNKS),
            dma(3), dma(3), dma(3, CHUNKS), dma(3, CHUNKS), dma(2, CHUNKS), dma(CHUNKS),
            dma(3, CHUNKS), dma(3, CHUNKS), dma(2, CHUNKS), dma(CHUNKS),
            dma(max(half_t - 1, 1), CHUNKS), dma(max(half_t - 1, 1), CHUNKS),
            dma(half_t, CHUNKS), dma(half_t, CHUNKS),
        ],
        compiler_params=pltpu.CompilerParams(collective_id=0, has_side_effects=True),
    )(queries, keys, values, mem_queries, mem_proj, mem_decay, pattern, grad_out)


def solution(mesh):
    cut = P("seq", "tensor")
    placed = (cut, cut, cut, P(None, "tensor"), P(None, "tensor"), cut, P("seq", None, None), cut)
    return jax.shard_map(
        functools.partial(local, mesh.shape["seq"], mesh.shape["tensor"]),
        mesh=mesh,
        in_specs=placed,
        out_specs=(cut, cut, cut, cut),
        check_vma=False,
    )
```

```python
import functools

import jax
import jax.numpy as jnp
from jax import lax
from jax.experimental import pallas as pl
from jax.experimental.pallas import tpu as pltpu
from jax.sharding import PartitionSpec as P

HD = 128
MEM = 128
BLOCK = 128
EPSILON = 1e-06
DEAD = -1e30
CHUNKS = 4
SCALE = HD ** (-0.5)
F32 = jnp.float32
BF16 = jnp.bfloat16

NN = (((1,), (0,)), ((), ()))
NT = (((1,), (1,)), ((), ()))
TN = (((0,), (0,)), ((), ()))


def dot(a, b, dims):
    return lax.dot_general(a, b, dims, preferred_element_type=F32)


def heads_loop(first, last, step, fn):
    if first >= last:
        return

    def lap(i, _):
        for j in range(step):
            fn(first + i * step + j)
        return 0

    lax.fori_loop(0, (last - first) // step, lap, 0)


def kernel(
    seqs, tensors,
    q_hbm, k_hbm, v_hbm, mq_hbm, mp_hbm, decay_ref, pattern_ref, do_hbm,
    o_hbm, gq_hbm, gk_ref, gv_ref,
    q_v, k_v, v_v, mq_v, mp_v, do_v, o_v, gq_v,
    rp_v, rw_v, sum_v, bias_v, mbias_v,
    p_v, dp_v, m_v, l_v, dd_v, pm_v, dsm_v, coef_v, row_v,
    core_send, core_recv, own_part, x_send, x_recv,
    dec_own, dec_peer, w_own, w_peer, e_send, e_recv,
    state_v, mk_v, mv_v, dmk_v, dmv_v, ds_own, ds_peer, b_send, b_recv,
    r_own, ag_x, ag_core, dsum_v, dk_v, dv_v,
    load_sem, store_sem,
    core_s, core_r, x_s, x_r, dec_s, dec_r, y_s, y_r, z_s, z_r,
    by_s, by_r, bz_s, bz_r, ax_s, ax_r, ac_s, ac_r,
):
    seg = k_v.shape[0]
    group = q_v.shape[1] // HD
    width = own_part.shape[2]
    rows = MEM // CHUNKS
    half_t, groups = tensors // 2, seqs // 4
    si, ti = lax.axis_index("seq"), lax.axis_index("tensor")
    gi, ri, yi = si // 4, (si // 2) % 2, si % 2
    xi, ci = ti // 2, ti % 2
    y, r = yi.astype(F32), ri.astype(F32)
    n_y, n_r = 1.0 - y, 1.0 - r
    core_dev = {"seq": si, "tensor": xi * 2 + (1 - ci)}
    y_dev = {"seq": gi * 4 + ri * 2 + (1 - yi), "tensor": ti}
    row_devs = [{"seq": gi * 4 + (1 - ri) * 2 + where, "tensor": ti} for where in (yi, 1 - yi)]
    group_devs = [y_dev] + row_devs
    after, before = (gi + 1) % groups, (gi + groups - 1) % groups
    up_devs = [{"seq": after * 4 + row * 2 + yi, "tensor": ti} for row in (1, 0)]
    down_devs = [{"seq": before * 4 + row * 2 + yi, "tensor": ti} for row in (0, 1)]
    x_devs = [{"seq": si, "tensor": ((xi + 1 + n) % half_t) * 2 + ci} for n in range(half_t - 1)]
    has_down, has_up = gi > 0, gi < groups - 1
    sends_up, sends_down = has_up & (ri == 1), has_down & (ri == 0)

    def remote(src, dst, send, recv, device):
        return pltpu.make_async_remote_copy(
            src_ref=src, dst_ref=dst, send_sem=send, recv_sem=recv,
            device_id=device, device_id_type=pl.DeviceIdType.MESH,
        )

    def head(h):
        return pl.ds(pl.multiple_of(h * HD, HD), HD)

    loads = [
        pltpu.make_async_copy(src, dst, load_sem.at[n])
        for n, (src, dst) in enumerate(
            ((k_hbm, k_v), (mq_hbm, mq_v), (v_hbm, v_v), (mp_hbm, mp_v), (q_hbm, q_v), (do_hbm, do_v))
        )
    ]
    for load in loads:
        load.start()
    barrier = pltpu.get_barrier_semaphore()

    def greet(device):
        pl.semaphore_signal(barrier, inc=1, device_id=device, device_id_type=pl.DeviceIdType.MESH)

    greet(core_dev)
    for device in group_devs + x_devs:
        greet(device)

    @pl.when(has_down)
    def _():
        greet(down_devs[1])

    @pl.when(has_up)
    def _():
        greet(up_devs[1])

    dec_own[...] = jnp.broadcast_to(decay_ref[...], dec_own.shape)

    tiles = seg // BLOCK
    tile_row = lax.broadcasted_iota(jnp.int32, (BLOCK, BLOCK), 0)
    tile_col = lax.broadcasted_iota(jnp.int32, (BLOCK, BLOCK), 1)
    diagonal = jnp.where(tile_row <= tile_col, 0.0, DEAD)
    zero_tile = jnp.zeros((BLOCK, BLOCK), F32)
    for b in range(tiles):
        at_b = slice(b * BLOCK, (b + 1) * BLOCK)
        off = (1.0 - pattern_ref[0, b, 0].astype(F32)) * DEAD
        mbias_v[:, at_b] = jnp.zeros((8, BLOCK), F32) + off
        for j in range(tiles):
            at_j = slice(j * BLOCK, (j + 1) * BLOCK)
            if j > b:
                bias_v[at_j, at_b] = zero_tile + DEAD
            else:
                off = (1.0 - pattern_ref[0, b, 1 + j].astype(F32)) * DEAD
                bias_v[at_j, at_b] = (diagonal if j == b else zero_tile) + off

    for load in loads[:3]:
        load.wait()

    def read_head(h):
        scores = dot(k_v[...], mq_v[:, head(h)], NT) * SCALE
        raised = jnp.exp(scores - jnp.max(scores, axis=0, keepdims=True))
        probs = raised / jnp.sum(raised, axis=0, keepdims=True)
        rp_v[h] = probs
        weights = probs.astype(BF16)
        rw_v[h] = weights
        sum_v[:, head(h)] = dot(weights, v_v[...], TN).astype(BF16)

    heads_loop(0, group, 4, read_head)
    loads[3].wait()

    def proj_rows(block):
        return mp_v[pl.ds(pl.multiple_of(block * width, width), width), :]

    chained = 2 * (ri * jnp.minimum(groups - 1 - gi, 1) + (1 - ri) * jnp.minimum(gi, 1))
    pl.semaphore_wait(barrier, 1 + len(group_devs) + len(x_devs) + chained)

    sent = []
    row_sent = []
    row_back = []
    up_sent = []
    down_sent = []

    def send(*args):
        copy = remote(*args)
        copy.start()
        sent.append(copy)

    def row_pair(own, peers, send_sems, recv_sems, c):
        return [
            remote(own.at[c], peers.at[1 + n, c], send_sems.at[1 + n, c], recv_sems.at[1 + n, c], row_devs[n])
            for n in range(2)
        ]

    for n, device in enumerate(group_devs):
        send(dec_own, dec_peer.at[n], dec_s.at[n], dec_r.at[n], device)

    for n in range(half_t):
        there = (xi + 1 + n) % half_t
        core_send[n] = dot(sum_v[...], proj_rows(there * 2 + (1 - ci)), NT)
        send(core_send.at[n], core_recv.at[n], core_s.at[n], core_r.at[n], core_dev)
    for n in range(half_t):
        there = (xi + 1 + n) % half_t
        own_part[n] = dot(sum_v[...], proj_rows(there * 2 + ci), NT)
    for n in range(half_t - 1):
        remote(core_send.at[n], core_recv.at[n], core_s.at[n], core_r.at[n], core_dev).wait_recv()
        for c in range(CHUNKS):
            at = slice(c * rows, (c + 1) * rows)
            x_send[n, c] = own_part[n, at, :] + core_recv[n, at, :]
            send(x_send.at[n, c], x_recv.at[n, c], x_s.at[n, c], x_r.at[n, c], x_devs[n])

    loads[4].wait()
    loads[5].wait()

    def own_head(h):
        scores = dot(k_v[...], q_v[:, head(h)], NT) * SCALE + bias_v[...]
        top = jnp.max(scores, axis=0, keepdims=True)
        raised = jnp.exp(scores - top)
        d_probs = dot(v_v[...], do_v[:, head(h)], NT)
        p_v[h] = raised
        dp_v[h] = d_probs
        m_v[h] = top
        l_v[h] = jnp.sum(raised, axis=0, keepdims=True)
        dd_v[h] = jnp.sum(raised * d_probs, axis=0, keepdims=True)

    heads_loop(0, group // 2, 2, own_head)

    last = half_t - 1
    remote(core_send.at[last], core_recv.at[last], core_s.at[last], core_r.at[last], core_dev).wait_recv()
    for c in range(CHUNKS):
        at = slice(c * rows, (c + 1) * rows)
        total = own_part[last, at, :] + core_recv[last, at, :]
        for n in range(half_t - 1):
            remote(x_send.at[n, c], x_recv.at[n, c], x_s.at[n, c], x_r.at[n, c], x_devs[n]).wait_recv()
            total = total + x_recv[n, c]
        w_own[c] = total
        send(w_own.at[c], w_peer.at[0, c], y_s.at[0, c], y_r.at[0, c], y_dev)
        row_copies = row_pair(w_own, w_peer, y_s, y_r, c)

        @pl.when(ri == 0)
        def _():
            for copy in row_copies:
                copy.start()

        row_sent.extend(row_copies)

    heads_loop(group // 2, group, 2, own_head)

    for n, device in enumerate(group_devs):
        remote(dec_own, dec_peer.at[n], dec_s.at[n], dec_r.at[n], device).wait_recv()
    mine, peer, same, cross = dec_own[0:1, :], dec_peer[0, 0:1, :], dec_peer[1, 0:1, :], dec_peer[2, 0:1, :]
    both, other = mine * peer, same * cross

    @pl.when(gi == 0)
    def _():
        e_recv[...] = jnp.zeros_like(e_recv)

    @pl.when(ri == 0)
    def _():
        w_peer[1] = jnp.zeros(w_peer.shape[1:], F32)
        w_peer[2] = jnp.zeros(w_peer.shape[1:], F32)

    for c in range(CHUNKS):
        at = slice(c * rows, (c + 1) * rows)
        remote(w_own.at[c], w_peer.at[0, c], y_s.at[0, c], y_r.at[0, c], y_dev).wait_recv()
        row_copies = row_pair(w_own, w_peer, y_s, y_r, c)

        @pl.when(ri == 1)
        def _():
            for copy in row_copies:
                copy.wait_recv()

        from_peer = w_peer[0, c]
        pair = (n_y * peer + y) * w_own[c] + (n_y + y * mine) * from_peer
        earlier = (n_y * cross + y) * w_peer[1, c] + (n_y + y * same) * w_peer[2, c]
        chain = [remote(e_send.at[c], e_recv.at[c], z_s.at[n, c], z_r.at[c], up_devs[n]) for n in range(2)]

        @pl.when(has_down)
        def _():
            chain[0].wait_recv()

        entering = (n_r + r * other) * e_recv[c] + r * earlier
        e_send[c] = both * entering + pair

        @pl.when(sends_up)
        def _():
            for copy in chain:
                copy.start()

        up_sent.extend(chain)
        state = (n_y + y * peer) * entering + y * from_peer
        state_v[at, :] = state
        for part, out in ((0, mk_v), (1, mv_v)):
            grid = state[:, part * HD : (part + 1) * HD]
            inv = lax.rsqrt(jnp.mean(grid * grid, axis=-1, keepdims=True) + EPSILON)
            out[at, :] = (grid * inv).astype(BF16)

    dmk_v[...] = jnp.zeros_like(dmk_v)
    dmv_v[...] = jnp.zeros_like(dmv_v)

    def memory_head(h):
        q_h, do_h = q_v[:, head(h)], do_v[:, head(h)]
        scores = dot(mk_v[...], q_h, NT) * SCALE + mbias_v[0:1, :]
        own_top = m_v[h]
        top = jnp.maximum(own_top, jnp.max(scores, axis=0, keepdims=True))
        shrink = jnp.exp(own_top - top)
        raised = jnp.exp(scores - top)
        inv = 1.0 / (shrink * l_v[h] + jnp.sum(raised, axis=0, keepdims=True))
        probs = raised * inv
        coef = shrink * inv
        d_probs = dot(mv_v[...], do_h, NT)
        row = coef * dd_v[h] + jnp.sum(probs * d_probs, axis=0, keepdims=True)
        d_scores = (probs * (d_probs - row) * SCALE).astype(BF16)
        weights = probs.astype(BF16)
        pm_v[h] = weights
        dsm_v[h] = d_scores
        coef_v[h] = coef
        row_v[h] = row
        dmk_v[...] += dot(d_scores, q_h, NN)
        dmv_v[...] += dot(weights, do_h, NN)

    heads_loop(0, group, 4, memory_head)

    d_state = []
    for part, grad in ((0, dmk_v), (1, dmv_v)):
        grid = state_v[:, part * HD : (part + 1) * HD]
        inv = lax.rsqrt(jnp.mean(grid * grid, axis=-1, keepdims=True) + EPSILON)
        d_normed = grad[...]
        mean = jnp.mean(d_normed * grid, axis=-1, keepdims=True)
        d_state.append(inv * d_normed - grid * (inv * inv * inv * mean))
    for c in range(CHUNKS):
        at = slice(c * rows, (c + 1) * rows)
        for part in range(2):
            ds_own[c, :, part * HD : (part + 1) * HD] = d_state[part][at, :]
        send(ds_own.at[c], ds_peer.at[0, c], by_s.at[0, c], by_r.at[0, c], y_dev)
        row_copies = row_pair(ds_own, ds_peer, by_s, by_r, c)

        @pl.when(ri == 1)
        def _():
            for copy in row_copies:
                copy.start()

        row_back.extend(row_copies)

    dk_v[...] = jnp.zeros_like(dk_v)
    dv_v[...] = jnp.zeros_like(dv_v)

    def grad_head(h):
        q_h, do_h = q_v[:, head(h)], do_v[:, head(h)]
        probs = p_v[h] * coef_v[h]
        d_scores = (probs * (dp_v[h] - row_v[h]) * SCALE).astype(BF16)
        weights = probs.astype(BF16)
        o_v[:, head(h)] = (dot(weights, v_v[...], TN) + dot(pm_v[h], mv_v[...], TN)).astype(BF16)
        gq_v[:, head(h)] = (dot(d_scores, k_v[...], TN) + dot(dsm_v[h], mk_v[...], TN)).astype(BF16)
        dk_v[...] += dot(d_scores, q_h, NN)
        dv_v[...] += dot(weights, do_h, NN)

    heads_loop(0, group // 2, 2, grad_head)

    @pl.when(gi == groups - 1)
    def _():
        b_recv[...] = jnp.zeros_like(b_recv)

    @pl.when(ri == 1)
    def _():
        ds_peer[1] = jnp.zeros(ds_peer.shape[1:], F32)
        ds_peer[2] = jnp.zeros(ds_peer.shape[1:], F32)

    for c in range(CHUNKS):
        remote(ds_own.at[c], ds_peer.at[0, c], by_s.at[0, c], by_r.at[0, c], y_dev).wait_recv()
        row_copies = row_pair(ds_own, ds_peer, by_s, by_r, c)

        @pl.when(ri == 0)
        def _():
            for copy in row_copies:
                copy.wait_recv()

        from_peer = ds_peer[0, c]
        pair = (y * peer + n_y) * ds_own[c] + (n_y * mine + y) * from_peer
        later = (y * cross + n_y) * ds_peer[1, c] + (n_y * same + y) * ds_peer[2, c]
        chain = [remote(b_send.at[c], b_recv.at[c], bz_s.at[n, c], bz_r.at[c], down_devs[n]) for n in range(2)]

        @pl.when(has_up)
        def _():
            chain[0].wait_recv()

        entering = (r + n_r * other) * b_recv[c] + n_r * later
        b_send[c] = pair + both * entering

        @pl.when(sends_down)
        def _():
            for copy in chain:
                copy.start()

        down_sent.extend(chain)
        at = slice(c * rows, (c + 1) * rows)
        r_own[at, :] = (y + n_y * peer) * entering + n_y * from_peer
        for n in range(half_t - 1):
            send(r_own.at[pl.ds(c * rows, rows)], ag_x.at[n, pl.ds(c * rows, rows)], ax_s.at[n, c], ax_r.at[n, c], x_devs[n])
        send(r_own.at[pl.ds(c * rows, rows)], ag_core.at[0, pl.ds(c * rows, rows)], ac_s.at[0, c], ac_r.at[0, c], core_dev)

    heads_loop(group // 2, group, 2, grad_head)
    stores = [
        pltpu.make_async_copy(o_v, o_hbm, store_sem.at[0]),
        pltpu.make_async_copy(gq_v, gq_hbm, store_sem.at[1]),
    ]
    for store in stores:
        store.start()

    def back(part, block):
        high = part.astype(BF16)
        low = (part - high.astype(F32)).astype(BF16)
        proj = proj_rows(block)
        return dot(high, proj, NN) + dot(low, proj, NN)

    total = back(r_own[...], ti)
    for n in range(half_t - 1):
        for c in range(CHUNKS):
            at = pl.ds(c * rows, rows)
            remote(r_own.at[at], ag_x.at[n, at], ax_s.at[n, c], ax_r.at[n, c], x_devs[n]).wait_recv()
            send(ag_x.at[n, at], ag_core.at[1 + n, at], ac_s.at[1 + n, c], ac_r.at[1 + n, c], core_dev)
    for n in range(half_t):
        for c in range(CHUNKS):
            at = pl.ds(c * rows, rows)
            remote(r_own.at[at], ag_core.at[n, at], ac_s.at[n, c], ac_r.at[n, c], core_dev).wait_recv()
        block = (xi + half_t - n) % half_t
        total = total + back(ag_core[n], block * 2 + (1 - ci))
        if n > 0:
            total = total + back(ag_x[n - 1], block * 2 + ci)
    dsum_v[...] = total.astype(BF16)

    def back_head(h):
        d_sum = dsum_v[:, head(h)]
        probs = rp_v[h]
        d_probs = dot(v_v[...], d_sum, NT)
        d_scores = probs * (d_probs - jnp.sum(probs * d_probs, axis=0, keepdims=True)) * SCALE
        dk_v[...] += dot(d_scores.astype(BF16), mq_v[:, head(h)], NN)
        dv_v[...] += dot(rw_v[h], d_sum, NN)

    heads_loop(0, group, 4, back_head)
    gk_ref[...] = dk_v[...].astype(BF16)
    gv_ref[...] = dv_v[...].astype(BF16)

    for copy in sent:
        copy.wait_send()
    for ends, copies in (
        (sends_up, up_sent), (sends_down, down_sent), (ri == 0, row_sent), (ri == 1, row_back)
    ):
        @pl.when(ends)
        def _():
            for copy in copies:
                copy.wait_send()

    for store in stores:
        store.wait()


def store_out(*refs):
    sources, targets, held, (load_sem, store_sem) = refs[:4], refs[4:8], refs[8:12], refs[12:]
    loads, stores = [], []
    for n in range(4):
        part = sources[n].shape[0] // 2
        for i in range(2):
            at = pl.ds(i * part, part)
            loads.append(pltpu.make_async_copy(sources[n].at[at], held[n].at[at], load_sem.at[n, i]))
            stores.append(pltpu.make_async_copy(held[n].at[at], targets[n].at[at], store_sem.at[n, i]))
    for load in loads:
        load.start()
    for load, store in zip(loads, stores):
        load.wait()
        store.start()
    for store in stores:
        store.wait()


def local(seqs, tensors, queries, keys, values, mem_queries, mem_proj, mem_decay, pattern, grad_out):
    seg, cols = queries.shape
    width = mem_decay.shape[1]
    group = cols // HD
    half_t = tensors // 2
    rows = MEM // CHUNKS
    assert keys.shape[1] == HD and width == 2 * HD
    assert seqs % 4 == 0 and tensors % 2 == 0
    vmem = pl.BlockSpec(memory_space=pltpu.VMEM)
    anywhere = pl.BlockSpec(memory_space=pl.ANY)
    like = lambda a: pltpu.VMEM(a.shape, a.dtype)
    f32 = lambda *shape: pltpu.VMEM(shape, F32)
    b16 = lambda *shape: pltpu.VMEM(shape, BF16)
    dma = lambda *shape: pltpu.SemaphoreType.DMA(shape)
    chunk = f32(CHUNKS, rows, width)
    chunks3 = f32(3, CHUNKS, rows, width)
    shapes = tuple(jax.ShapeDtypeStruct(a.shape, BF16) for a in (grad_out, queries, keys, values))
    results = pl.pallas_call(
        functools.partial(kernel, seqs, tensors),
        out_shape=shapes,
        in_specs=[
            anywhere, anywhere, anywhere, anywhere, anywhere, vmem,
            pl.BlockSpec(memory_space=pltpu.SMEM), anywhere,
        ],
        out_specs=(anywhere, anywhere, vmem, vmem),
        scratch_shapes=[
            like(queries), like(keys), like(values), like(mem_queries), like(mem_proj),
            like(grad_out), like(grad_out), like(queries),
            f32(group, seg, MEM), b16(group, seg, MEM), like(mem_queries), f32(seg, seg), f32(8, seg),
            f32(group, seg, seg), f32(group, seg, seg),
            f32(group, 1, seg), f32(group, 1, seg), f32(group, 1, seg),
            b16(group, MEM, seg), b16(group, MEM, seg), f32(group, 1, seg), f32(group, 1, seg),
            f32(half_t, MEM, width), f32(half_t, MEM, width), f32(half_t, MEM, width),
            f32(max(half_t - 1, 1), CHUNKS, rows, width), f32(max(half_t - 1, 1), CHUNKS, rows, width),
            f32(8, width), f32(3, 8, width), chunk, chunks3, chunk, chunk,
            f32(MEM, width), b16(MEM, HD), b16(MEM, HD), f32(MEM, HD), f32(MEM, HD),
            chunk, chunks3, chunk, chunk,
            f32(MEM, width), f32(max(half_t - 1, 1), MEM, width), f32(half_t, MEM, width),
            like(mem_queries), f32(seg, HD), f32(seg, HD),
            dma(6), dma(2),
            dma(half_t), dma(half_t),
            dma(max(half_t - 1, 1), CHUNKS), dma(max(half_t - 1, 1), CHUNKS),
            dma(3), dma(3), dma(3, CHUNKS), dma(3, CHUNKS), dma(2, CHUNKS), dma(CHUNKS),
            dma(3, CHUNKS), dma(3, CHUNKS), dma(2, CHUNKS), dma(CHUNKS),
            dma(max(half_t - 1, 1), CHUNKS), dma(max(half_t - 1, 1), CHUNKS),
            dma(half_t, CHUNKS), dma(half_t, CHUNKS),
        ],
        compiler_params=pltpu.CompilerParams(collective_id=0, has_side_effects=True),
    )(queries, keys, values, mem_queries, mem_proj, mem_decay, pattern, grad_out)
    return pl.pallas_call(
        store_out,
        out_shape=shapes,
        in_specs=[anywhere] * 4,
        out_specs=(anywhere,) * 4,
        scratch_shapes=[like(a) for a in shapes] + [dma(4, 2), dma(4, 2)],
    )(*results)


def solution(mesh):
    cut = P("seq", "tensor")
    placed = (cut, cut, cut, P(None, "tensor"), P(None, "tensor"), cut, P("seq", None, None), cut)
    return jax.shard_map(
        functools.partial(local, mesh.shape["seq"], mesh.shape["tensor"]),
        mesh=mesh,
        in_specs=placed,
        out_specs=(cut, cut, cut, cut),
        check_vma=False,
    )
```
